32 devices in a mesh: section: 8 (over y, x, core), latent: 4 (over z).
Axes of the slice: x: 2, y: 2, z: 4, core: 2. Of those that a mesh axis runs over, the one named last changes fastest.
Arguments:
- token_ids: int32 [1024], replicated, may hold values from 0 to 15
- embedded: bfloat16 [1024, 3584], P('latent'), may hold values from -6 to 6
- deltas: bfloat16 [8, 1024, 3584], P('section', 'latent'), may hold values from -6 to 6
- enc_weight: bfloat16 [8, 3584, 4096], P('section', None, 'latent'), may hold values from -0.015625 to 0.015625
- enc_bias: float32 [4096], P('latent'), may hold values from -1.5 to 0.5
- dec_weight: bfloat16 [8, 4096, 3584], P('section', 'latent'), may hold values from -0.09375 to 0.09375
- dec_bias: float32 [8, 3584], P('section'), may hold values from -3 to 3
Outputs:
- latents: bfloat16 [1024, 4096], P('section', 'latent')
- recon: bfloat16 [8, 1024, 3584], P('section', 'latent')
- losses: float32 [2], replicated
The draws below stay inside these ranges and needn't reach their ends.
All inputs are finite; a program needn't handle non-finite values.
Results may differ from the reference program's by a relative error of at most 0.012.
Values may be sent and summed in bfloat16 or wider, within the bound.
No kernel may reach another device: no remote copies, remote signals or barrier semaphores. Data moves between devices by JAX's collectives and lax.ppermute only.
A program may use at most 128 MiB of HBM per device.

```python
import jax
import jax.numpy as jnp
from jax import lax

D = 3584
TOKENS = 1024
F = 4096
LAYERS = 8
N_SECTION = 8


def plant(result, stream_key, smallest, top_value):
    longest = result.shape.index(max(result.shape))
    spots = []
    for shift in (0, 1):
        where = [jax.random.randint(jax.random.fold_in(stream_key, axis), (), 0, length) for axis, length in enumerate(result.shape)]
        where[longest] = (where[longest] + shift) % result.shape[longest]
        spots.append(tuple(where))
    return result.at[spots[0]].set(smallest).at[spots[1]].set(top_value)


def block_levels(rng, shape, split, smallest, largest):
    gain, own = 1.0, jax.random.fold_in(rng, 6)
    for axis_at, parts in split:
        heights = jnp.exp(jax.random.uniform(jax.random.fold_in(own, axis_at), (parts,), jnp.float32, smallest / len(split), largest / len(split)))
        gain = gain * jnp.repeat(heights, shape[axis_at] // parts).reshape([-1 if axis == axis_at else 1 for axis in range(len(shape))])
    return gain


def bell_draw(rng, shape, scale, limit, pieces=(), dtype=jnp.bfloat16):
    drawn = scale * jax.random.normal(rng, shape, jnp.float32)
    if pieces:
        drawn = drawn * block_levels(rng, shape, pieces, -0.22, 0.18)
    return jnp.clip(drawn, -limit, limit).astype(dtype)


def setup_inputs(seed: int = 0) -> dict:
    key_of = jax.random.split(jax.random.key(seed), 8)
    token_ids = plant(jax.random.randint(key_of[0], (TOKENS,), 0, 16), jax.random.fold_in(key_of[0], 1), 0, 15).astype(jnp.int32)
    embedded = bell_draw(key_of[1], (TOKENS, D), 1.0, 6.0, ((0, 4),))
    deltas = bell_draw(key_of[2], (LAYERS, TOKENS, D), 1.0, 6.0, ((0, 8), (1, 4)))
    enc_weight = bell_draw(key_of[3], (LAYERS, D, F), (4 * D * LAYERS) ** -0.5, 0.015625, ((0, 8), (2, 4)))
    enc_bias = jnp.clip(-1.5 + 2.0 * jax.random.uniform(key_of[4], (F,), jnp.float32) ** block_levels(key_of[4], (F,), ((0, 4),), -0.2, 0.2), -1.5, 0.5)
    dec_weight = bell_draw(key_of[5], (LAYERS, F, D), F ** -0.5, 0.09375, ((0, 8), (1, 4)))
    dec_bias = bell_draw(key_of[6], (LAYERS, D), 0.5, 3.0, ((0, 8),), jnp.float32)
    return dict(token_ids=token_ids, embedded=embedded, deltas=deltas, enc_weight=enc_weight, enc_bias=enc_bias, dec_weight=dec_weight, dec_bias=dec_bias)


first_ordinary = 3

def reference(token_ids, embedded, deltas, enc_weight, enc_bias, dec_weight, dec_bias):
    keep_flags = (token_ids >= first_ordinary).astype(jnp.float32)
    stacked = jnp.cumsum(deltas.astype(jnp.float32), axis=0) + embedded.astype(jnp.float32)[None]
    residual = stacked.astype(jnp.bfloat16)

    def enc_step(totals, layer_pair):
        return (totals + jnp.dot(layer_pair[0], layer_pair[1], preferred_element_type=jnp.float32), None)
    pre_acts, _ = lax.scan(enc_step, jnp.zeros((TOKENS, F), jnp.float32), (residual, enc_weight))
    pre_acts = pre_acts + enc_bias.astype(jnp.float32)
    latents = (keep_flags[:, None] * jax.nn.relu(pre_acts)).astype(jnp.bfloat16)

    def dec_step(carried, layer_items):
        rebuilt = jnp.dot(latents, layer_items[1], preferred_element_type=jnp.float32) + layer_items[2].astype(jnp.float32)
        squared = jnp.sum(keep_flags[:, None] * jnp.square(layer_items[0].astype(jnp.float32) - rebuilt))
        col_norms = jnp.sqrt(lax.optimization_barrier(jnp.sum(jnp.square(layer_items[1].astype(jnp.float32)), axis=1)))
        return (carried, (rebuilt.astype(jnp.bfloat16), squared, col_norms))
    _, (recon, squares_all, norms_all) = lax.scan(dec_step, jnp.zeros((), jnp.float32), (residual, dec_weight, dec_bias))
    latent_sums = lax.optimization_barrier(jnp.sum(latents.astype(jnp.float32), axis=0))
    sparsity = jnp.sum(latent_sums * lax.optimization_barrier(jnp.sum(norms_all, axis=0)))
    losses = jnp.stack([jnp.sum(squares_all) / (TOKENS * N_SECTION * D), sparsity / (TOKENS * F)])
    return (latents, recon, losses)
```

```python
import jax
import jax.numpy as jnp
from jax import lax
from jax.sharding import PartitionSpec as P

first_ordinary = 3
n_chunks = 2


f32 = jnp.float32
bf16 = jnp.bfloat16


def bits_of(count):
    return [1 << j for j in range(count.bit_length() - 1)]


def swap(x, axis, mask):
    count = lax.axis_size(axis)
    return lax.ppermute(x, axis, [(i, i ^ mask) for i in range(count)])


def line_links(count):
    even = [(i, i + 1) for i in range(0, count - 1, 2)]
    odd = [(i, i + 1) for i in range(1, count - 1, 2)]
    return even, odd


def rows_at(x, start, count):
    return lax.dynamic_slice_in_dim(x, start, count, 0)


def halves(mine, other, core):
    first = jnp.where(core == 0, mine, other)
    second = jnp.where(core == 0, other, mine)
    return jnp.concatenate([first, second], axis=0)


def residual_chunk(embedded, delta, low, count, sect, core):
    half = count // 2
    mine_at = low + core * half
    other_at = low + (1 - core) * half
    d_mine = rows_at(delta, mine_at, half)
    d_pair = swap(rows_at(delta, other_at, half), "section", 1).astype(f32)
    d_mine = d_mine.astype(f32)
    pair = d_mine + d_pair
    total = pair
    base = rows_at(embedded, mine_at, half).astype(f32)
    for mask in bits_of(lax.axis_size("section"))[1:]:
        got = swap(total.astype(bf16), "section", mask).astype(f32)
        base = base + jnp.where((sect & mask) != 0, got, 0.0)
        total = total + got
    lower = (base + jnp.where(core == 0, d_mine, d_pair)).astype(bf16)
    upper = (base + pair).astype(bf16)
    mine = jnp.where(core == 0, lower, upper)
    give = jnp.where(core == 0, upper, lower)
    return halves(mine, swap(give, "section", 1), core)


class Line:
    def __init__(self, axis):
        self.axis = axis
        self.place = lax.axis_index(axis)
        count = lax.axis_size(axis)
        self.count = count
        self.inner = (self.place > 0) & (self.place < count - 1)
        self.left = self.place < count // 2

    def block(self, mirrored):
        return jnp.where(self.left, mirrored, self.count - 1 - mirrored)

    def blocks(self):
        beside = self.place ^ 1
        return [self.place, beside, self.block(2), self.block(3)]

    def even(self, x):
        return lax.ppermute(x, self.axis, [(0, 1), (1, 0), (2, 3), (3, 2)])

    def inward(self, x):
        return lax.ppermute(x, self.axis, [(0, 1), (3, 2)])

    def outward(self, x):
        return lax.ppermute(x, self.axis, [(1, 0), (2, 3)])

    def odd(self, x):
        return lax.ppermute(x, self.axis, [(1, 2), (2, 1)])

    def gather(self, own):
        a1 = self.even(own)
        b1 = self.odd(own)
        a2 = self.outward(b1)
        b2 = self.odd(a1)
        a3 = self.outward(b2)
        third = jnp.where(self.inner, b1, a2)
        fourth = jnp.where(self.inner, b2, a3)
        return [own, a1, third, fourth]

    def scatter(self, parts):
        own, beside, third, fourth = parts
        r1 = self.inward(fourth.astype(bf16))
        r2a = self.inward(third.astype(bf16))
        r2b = self.odd((fourth + r1.astype(f32)).astype(bf16))
        r3a = self.even((beside + r2b.astype(f32)).astype(bf16))
        r3b = self.odd((third + r2a.astype(f32)).astype(bf16))
        return own + r3a.astype(f32) + r3b.astype(f32)


class Whole:
    def __init__(self, axis):
        self.axis = axis
        self.count = lax.axis_size(axis)

    def blocks(self):
        return list(range(self.count))

    def gather(self, own):
        every = lax.all_gather(own, self.axis)
        return [every[k] for k in range(self.count)]

    def scatter(self, parts):
        every = jnp.concatenate([part.astype(bf16) for part in parts], axis=0)
        return lax.psum_scatter(every, self.axis, scatter_dimension=0, tiled=True).astype(f32)


def reduce_group(pre, keep, bias, core):
    half = pre.shape[0] // 2
    total = rows_at(pre, core * half, half)
    give = rows_at(pre, (1 - core) * half, half).astype(bf16)
    total = total + swap(give, "section", 1).astype(f32)
    for mask in bits_of(lax.axis_size("section"))[1:]:
        total = total + swap(total.astype(bf16), "section", mask).astype(f32)
    flags = rows_at(keep, core * half, half)
    mine = (flags[:, None] * jax.nn.relu(total + bias)).astype(bf16)
    return halves(mine, swap(mine, "section", 1), core)


def local(token_ids, embedded, deltas, enc_weight, enc_bias, dec_weight, dec_bias):
    rows = embedded.shape[0]
    n_section, n_latent = lax.axis_size("section"), lax.axis_size("latent")
    sect = lax.axis_index("section")
    place = lax.axis_index("latent")
    core = sect & 1
    delta, enc, dec, bias_out = deltas[0], enc_weight[0], dec_weight[0], dec_bias[0]
    keep = (token_ids >= first_ordinary).astype(f32)
    line = Line("latent") if n_latent == 4 else Whole("latent")
    blocks = line.blocks()
    step = rows // n_chunks
    col_norms = jnp.sqrt(jnp.sum(jnp.square(dec.astype(f32)), axis=1))

    squared = jnp.zeros((), f32)
    latent_sums = jnp.zeros((dec.shape[0],), f32)
    recon_chunks = []
    latent_chunks = []
    for c in range(n_chunks):
        low = c * step
        residual = residual_chunk(embedded, delta, low, step, sect, core)
        slots = line.gather(residual)
        groups = [list(range(len(slots) - 1)), [len(slots) - 1]] if n_latent == 4 else [list(range(len(slots)))]
        latents = {}
        for group in groups:
            pre = jnp.concatenate([jnp.dot(slots[k], enc, preferred_element_type=f32) for k in group], axis=0)
            flags = jnp.concatenate([rows_at(keep, blocks[k] * rows + low, step) for k in group], axis=0)
            out = reduce_group(pre, flags, enc_bias, core)
            latent_sums = latent_sums + jnp.sum(out.astype(f32), axis=0)
            for at, k in enumerate(group):
                latents[k] = out[at * step : (at + 1) * step]
        latent_chunks.append(latents)

        parts = [jnp.dot(latents[k], dec, preferred_element_type=f32) for k in range(len(slots))]
        rebuilt = line.scatter(parts) + bias_out[None]
        keep_own = rows_at(keep, place * rows + low, step)
        squared = squared + jnp.sum(keep_own[:, None] * jnp.square(residual.astype(f32) - rebuilt))
        recon_chunks.append(rebuilt.astype(bf16))

    recon = jnp.concatenate(recon_chunks, axis=0)
    share = n_latent * rows // n_section
    first = sect * share
    ordered = jnp.concatenate([latent_chunks[c][k] for k in range(n_latent) for c in range(n_chunks)], axis=0)
    slot = jnp.zeros((), jnp.int32)
    for k in range(n_latent):
        slot = jnp.where(blocks[k] == first // rows, k, slot)
    own_latents = rows_at(ordered, slot * rows + first % rows, share)

    sparsity = jnp.sum(latent_sums * col_norms)
    lane = lax.broadcasted_iota(jnp.int32, (8, 128), 1)
    sums = jnp.where(lane == 0, squared, jnp.where(lane == 1, sparsity, 0.0))
    for axis in ("latent", "section"):
        for mask in bits_of(lax.axis_size(axis)):
            sums = sums + swap(sums, axis, mask)
    token_total = n_latent * rows
    losses = jnp.stack(
        [
            sums[0, 0] / (token_total * n_section * dec.shape[1]),
            sums[0, 1] / (token_total * dec.shape[0] * n_latent),
        ]
    )
    return (own_latents, recon[None], losses)


def solution(mesh):
    in_specs = (
        P(),
        P("latent", None),
        P("section", "latent", None),
        P("section", None, "latent"),
        P("latent"),
        P("section", "latent", None),
        P("section", None),
    )
    out_specs = (P("section", "latent"), P("section", "latent", None), P())
    return jax.shard_map(local, mesh=mesh, in_specs=in_specs, out_specs=out_specs, check_vma=False)
```
